32 devices in a mesh: grp: 2 (over x), seq: 16 (over z, y, core).
Axes of the slice: x: 2, y: 2, z: 4, core: 2. Of those that a mesh axis runs over, the one named last changes fastest.
Arguments:
- fresh_query: bfloat16 [4096, 4096], P(('grp', 'seq')), parts along dimension 0, may hold values from -80 to 80
- fresh_key: bfloat16 [4096, 4096], P(('grp', 'seq')), parts along dimension 0, may hold values from -4 to 4
- fresh_value: bfloat16 [4096, 4096], P(('grp', 'seq')), parts along dimension 0, may hold values from -4 to 4
- stale_key: bfloat16 [8192, 4096], P('grp', 'seq'), parts along dimension 0, may hold values from -4 to 4
- stale_value: bfloat16 [8192, 4096], P('grp', 'seq'), parts along dimension 0, may hold values from -4 to 4
- patch_start: int32 [2], P('grp'), parts along dimension 0, may hold values from 0 to 2048
- timestep: int32 [2], P('grp'), parts along dimension 0, may hold values from 0 to 34
- gate_table: float32 [35, 4096], replicated, may hold values from -4 to 4
Outputs:
- gated: bfloat16 [4096, 4096], P(('grp', 'seq')), parts along dimension 0
The draws below stay inside these ranges and needn't reach their ends.
There are 2 independent parts, one for each index of `grp`. The reference program is written for one: setup_inputs(seed, part) draws one part's arguments, and reference() takes and returns one part's arrays. A program takes and returns all parts, laid end to end along the dimension named above; an argument that names none is the same for every part. Nothing has to cross between parts.
All inputs are finite; a program needn't handle non-finite values.
Results may differ from the reference program's by a relative error of at most 0.0056.
Values may be sent and summed in bfloat16 or wider, within the bound.
No kernel may reach another device: no remote copies, remote signals or barrier semaphores. Data moves between devices by JAX's collectives and lax.ppermute only.
A program may use at most 64 MiB of HBM per device.

```python
import jax
import jax.numpy as jnp
from jax import lax

D = 4096
HEADS = 32
HD = 128
PATCH = 2048
SEQ = 4096
STEPS = 35


def draw_fresh_query(key, part):
    own = jax.random.fold_in(key, 11)
    values = jnp.clip(jax.random.normal(own, (PATCH, D), jnp.float32), -4.0, 4.0)
    return values.astype(jnp.bfloat16)


def draw_fresh_key(key, part):
    own = jax.random.fold_in(key, 23)
    values = jnp.clip(jax.random.normal(own, (PATCH, D), jnp.float32), -4.0, 4.0)
    return values.astype(jnp.bfloat16)


def shard_levels(key, extent, pieces, least, top_value):
    factor_of, own = 1.0, jax.random.fold_in(key, 6)
    for dim, parts in pieces:
        heights = jnp.exp(jax.random.uniform(jax.random.fold_in(own, dim), (parts,), jnp.float32, least / len(pieces), top_value / len(pieces)))
        factor_of = factor_of * jnp.repeat(heights, extent[dim] // parts).reshape([-1 if axis == dim else 1 for axis in range(len(extent))])
    return factor_of


def centred(own_key, extent, deviation, limit, shards=(), kind=jnp.bfloat16):
    values = jax.random.normal(own_key, extent, jnp.float32) * deviation
    if len(shards) > 0:
        values = shard_levels(own_key, extent, shards, -0.22, 0.18) * values
    return jnp.clip(values, min=-limit, max=limit).astype(kind)


def setup_inputs(seed: int = 0, part: int = 0) -> dict:
    seeds = jax.random.split(jax.random.key(seed), 9)
    part_keys = jax.random.split(jax.random.fold_in(seeds[8], part), 9)
    return {
        "fresh_query": draw_fresh_query(jax.random.fold_in(jax.random.fold_in(seeds[8], part), 71), part),
        "fresh_key": draw_fresh_key(jax.random.fold_in(jax.random.fold_in(seeds[8], part), 71), part),
        "fresh_value": centred(part_keys[2], (PATCH, D), 1.0, 4.0, ((0, 16),)),
        "stale_key": centred(part_keys[3], (SEQ, D), 1.0, 4.0, ((1, 16),)),
        "stale_value": centred(part_keys[4], (SEQ, D), 1.0, 4.0, ((1, 16),)),
        "patch_start": jax.random.randint(part_keys[5], (1,), 0, SEQ - PATCH + 1).astype(jnp.int32),
        "timestep": jax.random.randint(part_keys[6], (1,), 0, STEPS).astype(jnp.int32),
        "gate_table": centred(seeds[7], (STEPS, D), 1.0, 4.0, (), jnp.float32),
    }


def attend_group(queries, keys, values):
    scores = jnp.dot(queries, keys.T, preferred_element_type=jnp.float32) * (HD ** -0.5)
    row_max = jnp.max(scores, axis=1)
    expo = jnp.exp(scores - row_max[:, None])
    total = jnp.sum(expo, axis=1)
    output = jnp.dot(expo.astype(jnp.bfloat16), values, preferred_element_type=jnp.float32)
    return row_max, total, output


def by_heads(array):
    return array.reshape(array.shape[0], HEADS, HD).transpose(1, 0, 2)


def reference(fresh_query, fresh_key, fresh_value, stale_key, stale_value, patch_start, timestep, gate_table):
    shift_by = -(patch_start[0] + PATCH)
    old_key = jnp.roll(stale_key, shift_by, axis=0)[: SEQ - PATCH]
    old_value = jnp.roll(stale_value, shift_by, axis=0)[: SEQ - PATCH]

    def one_head(packed):
        queries, new_key, new_value, key_old, value_old = packed
        max_old, sum_old, out_old = attend_group(queries, key_old, value_old)
        max_new, sum_new, out_new = attend_group(queries, new_key, new_value)
        top = jnp.maximum(max_old, max_new)
        scale_old = jnp.exp(max_old - top)
        scale_new = jnp.exp(max_new - top)
        numer = scale_old[:, None] * out_old + scale_new[:, None] * out_new
        denom = scale_old * sum_old + scale_new * sum_new
        return (numer / denom[:, None]).astype(jnp.bfloat16)

    heads_out = lax.map(one_head, (by_heads(fresh_query), by_heads(fresh_key), by_heads(fresh_value), by_heads(old_key), by_heads(old_value)))
    attn = heads_out.transpose(1, 0, 2).reshape(PATCH, D)
    gate_row = lax.dynamic_slice_in_dim(gate_table, timestep[0], 1, 0)
    return (attn.astype(jnp.float32) * gate_row).astype(jnp.bfloat16)
```

```python
import functools
import math

import jax
import jax.numpy as jnp
from jax import lax
from jax.experimental import pallas as pl
from jax.experimental.pallas import tpu as pltpu
from jax.sharding import PartitionSpec as P


HD = 128
TO_LOG2 = HD ** (-0.5) * math.log2(math.e)
NT = (((1,), (1,)), ((), ()))


def pack_first_body(heads_dev, q_ref, k_ref, v_ref, out_ref):
    rows = q_ref.shape[0]
    for dest in range(out_ref.shape[0]):
        base = dest * heads_dev * HD
        head0 = slice(base, base + HD)
        out_ref[dest, :rows] = q_ref[:, head0]
        out_ref[dest, rows : 2 * rows] = k_ref[:, head0]
        out_ref[dest, 2 * rows : 3 * rows] = v_ref[:, head0]
        for head in range(1, heads_dev):
            cols = slice(base + head * HD, base + (head + 1) * HD)
            out_ref[dest, (2 + head) * rows : (3 + head) * rows] = q_ref[:, cols]


def pack_first(q, k, v, n, heads_dev):
    rows, width = q.shape
    per = min(4, n)
    cols = per * heads_dev * HD
    src = pl.BlockSpec((rows, cols), lambda i: (0, i))
    return pl.pallas_call(
        functools.partial(pack_first_body, heads_dev),
        out_shape=jax.ShapeDtypeStruct((n, (2 + heads_dev) * rows, HD), q.dtype),
        grid=(n // per,),
        in_specs=[src, src, src],
        out_specs=pl.BlockSpec((per, (2 + heads_dev) * rows, HD), lambda i: (i, 0, 0)),
        cost_estimate=pl.CostEstimate(
            flops=0, bytes_accessed=2 * rows * width * 5, transcendentals=0
        ),
    )(q, k, v)


def pack_rest_body(heads_dev, me_ref, k_ref, v_ref, *out_refs):
    rows = k_ref.shape[0]
    for step, out_ref in enumerate(out_refs):
        dest = me_ref[0] ^ step
        for head in range(1, heads_dev):
            at = pl.multiple_of((dest * heads_dev + head) * HD, HD)
            out_ref[head - 1, :rows] = k_ref[:, pl.ds(at, HD)]
            out_ref[head - 1, rows:] = v_ref[:, pl.ds(at, HD)]


def pack_rest(me, k, v, n, heads_dev):
    rows, width = k.shape
    whole = pl.BlockSpec(memory_space=pltpu.VMEM)
    block = jax.ShapeDtypeStruct((heads_dev - 1, 2 * rows, HD), k.dtype)
    return pl.pallas_call(
        functools.partial(pack_rest_body, heads_dev),
        out_shape=[block] * n,
        in_specs=[pl.BlockSpec(memory_space=pltpu.SMEM), whole, whole],
        out_specs=[whole] * n,
        cost_estimate=pl.CostEstimate(
            flops=0, bytes_accessed=2 * rows * width * 3, transcendentals=0
        ),
    )(me, k, v)


def keep_old_body(scal_ref, k_low, k_high, v_low, v_high, k_ref, v_ref):
    rows = k_low.shape[0]
    at = lax.broadcasted_iota(jnp.int32, (rows, HD), 0) + pl.program_id(1) * rows
    before = at < scal_ref[1]
    for low, high, out_ref in ((k_low, k_high, k_ref), (v_low, v_high, v_ref)):
        kept = jnp.where(before, low[...].astype(jnp.float32), high[...].astype(jnp.float32))
        out_ref[0] = kept.astype(out_ref.dtype)


def keep_old(scal, stale_k, stale_v, patch, heads_dev):
    n_old = stale_k.shape[0] - patch
    rows = math.gcd(math.gcd(n_old, patch), 1024)
    low = pl.BlockSpec((rows, HD), lambda h, i, s: (i, h))
    high = pl.BlockSpec((rows, HD), lambda h, i, s: (i + patch // rows, h))
    out = pl.BlockSpec((1, rows, HD), lambda h, i, s: (h, i, 0))
    kept = jax.ShapeDtypeStruct((heads_dev, n_old, HD), stale_k.dtype)
    return pl.pallas_call(
        keep_old_body,
        out_shape=[kept, kept],
        grid_spec=pltpu.PrefetchScalarGridSpec(
            num_scalar_prefetch=1,
            grid=(heads_dev, n_old // rows),
            in_specs=[low, high, low, high],
            out_specs=[out, out],
        ),
        cost_estimate=pl.CostEstimate(
            flops=0, bytes_accessed=12 * heads_dev * n_old * HD, transcendentals=0
        ),
    )(scal, stale_k, stale_k, stale_v, stale_v)


def attend_body(rows, n_new_refs, scal_ref, q_ref, *refs):
    new_refs = refs[:n_new_refs]
    old_k_ref, old_v_ref, gate_ref, out_ref, keys, values = refs[n_new_refs:]
    total = keys.shape[0]
    n_old = old_k_ref.shape[1]
    patch = total - n_old

    @pl.when(pl.program_id(0) == 0)
    def _():
        keys[:n_old] = old_k_ref[0]
        values[:n_old, :HD] = old_v_ref[0]
        values[:, HD:] = jnp.ones((total, HD), jnp.bfloat16)
        if n_new_refs == 2:
            keys[n_old:] = new_refs[0][...].reshape(patch, HD)
            values[n_old:, :HD] = new_refs[1][...].reshape(patch, HD)
        else:
            for source, ref in enumerate(new_refs):
                at = slice(n_old + source * rows, n_old + (source + 1) * rows)
                keys[at] = ref[0, :rows]
                values[at, :HD] = ref[0, rows:]

    queries = q_ref[...].reshape(-1, HD)
    gate = gate_ref[pl.ds(scal_ref[2], 1), :]
    block = min(256, queries.shape[0])
    chunk = 512
    for start in range(0, queries.shape[0], block):
        q = queries[start : start + block]
        top, acc = None, None
        for at in range(0, total, chunk):
            s = lax.dot_general(
                q, keys[at : at + chunk], NT, preferred_element_type=jnp.float32
            )
            chunk_top = jnp.max(s, axis=1, keepdims=True)
            new_top = chunk_top if top is None else jnp.maximum(top, chunk_top)
            p = jnp.exp2((s - new_top) * TO_LOG2).astype(jnp.bfloat16)
            part = jnp.dot(p, values[at : at + chunk], preferred_element_type=jnp.float32)
            if top is None:
                acc = part
            else:
                acc = acc * jnp.exp2((top - new_top) * TO_LOG2) + part
            top = new_top
        attn = (acc[:, :HD] / acc[:, HD:]).astype(jnp.bfloat16)
        gated = (attn.astype(jnp.float32) * gate).astype(jnp.bfloat16)
        for part in range(block // rows):
            piece = gated[part * rows : (part + 1) * rows]
            out_ref[start // rows + part] = piece


def attend(scal, first, head, new_parts, old_k, old_v, gate_table, n, rows, heads_dev):
    per = min(4, n)
    n_old = old_k.shape[1]
    patch = n * rows
    total = n_old + patch
    q_at = 0 if head == 0 else 2 + head
    query = pl.BlockSpec((per, rows, HD), lambda i, s: (i, q_at, 0))
    if head == 0:
        new_ops = [first, first]
        new_specs = [
            pl.BlockSpec((n, rows, HD), lambda i, s: (0, 1, 0)),
            pl.BlockSpec((n, rows, HD), lambda i, s: (0, 2, 0)),
        ]
    else:
        new_ops = new_parts
        new_specs = [pl.BlockSpec((1, 2 * rows, HD), lambda i, s: (head - 1, 0, 0))] * n
    old = pl.BlockSpec((1, n_old, HD), lambda i, s: (head, 0, 0))
    gate = pl.BlockSpec(
        (gate_table.shape[0], HD), lambda i, s: (0, s[0] * heads_dev + head)
    )
    return pl.pallas_call(
        functools.partial(attend_body, rows, len(new_ops)),
        out_shape=jax.ShapeDtypeStruct((n, rows, HD), jnp.bfloat16),
        grid_spec=pltpu.PrefetchScalarGridSpec(
            num_scalar_prefetch=1,
            grid=(n // per,),
            in_specs=[query, *new_specs, old, old, gate],
            out_specs=pl.BlockSpec((per, rows, HD), lambda i, s: (i, 0, 0)),
            scratch_shapes=[
                pltpu.VMEM((total, HD), jnp.bfloat16),
                pltpu.VMEM((total, 2 * HD), jnp.bfloat16),
            ],
        ),
        compiler_params=pltpu.CompilerParams(vmem_limit_bytes=32 << 20),
        cost_estimate=pl.CostEstimate(
            flops=4 * patch * total * 2 * HD,
            bytes_accessed=2 * HD * (2 * patch + 2 * total),
            transcendentals=patch * total,
        ),
    )(scal, first, *new_ops, old_k, old_v, gate_table)


def unpack_body(heads_dev, *refs):
    out_ref = refs[-1]
    for source in range(refs[0].shape[0]):
        for head in range(heads_dev):
            at = (source * heads_dev + head) * HD
            out_ref[:, at : at + HD] = refs[head][source]


def unpack(parts, n, rows, heads_dev):
    per = min(4, n)
    src = pl.BlockSpec((per, rows, HD), lambda i: (i, 0, 0))
    return pl.pallas_call(
        functools.partial(unpack_body, heads_dev),
        out_shape=jax.ShapeDtypeStruct((rows, n * heads_dev * HD), parts[0].dtype),
        grid=(n // per,),
        in_specs=[src] * heads_dev,
        out_specs=pl.BlockSpec((rows, per * heads_dev * HD), lambda i: (0, i)),
    )(*parts)


def shards(
    fresh_query, fresh_key, fresh_value, stale_key, stale_value, patch_start, timestep, gate_table
):
    n = lax.axis_size("seq")
    rows = fresh_query.shape[0]
    heads_dev = stale_key.shape[1] // HD
    me = lax.axis_index("seq").astype(jnp.int32)
    scal = jnp.stack([me, patch_start[0], timestep[0]])
    exchange = functools.partial(
        lax.all_to_all, axis_name="seq", split_axis=0, concat_axis=0, tiled=True
    )
    packed = pack_first(fresh_query, fresh_key, fresh_value, n, heads_dev)
    first = exchange(packed)
    old_k, old_v = keep_old(scal, stale_key, stale_value, n * rows, heads_dev)
    rest = None
    if heads_dev > 1:
        blocks = pack_rest(me[None], fresh_key, fresh_value, n, heads_dev)
        rest = [blocks[0]]
        for step in range(1, n):
            pairs = [(i, i ^ step) for i in range(n)]
            rest.append(lax.ppermute(blocks[step], "seq", pairs))
    parts = []
    for head in range(heads_dev):
        gated = attend(
            scal, first, head, rest, old_k, old_v, gate_table,
            n, rows, heads_dev,
        )
        parts.append(exchange(gated))
    return unpack(parts, n, rows, heads_dev)


def solution(mesh):
    return jax.shard_map(
        shards,
        mesh=mesh,
        in_specs=(
            P(("grp", "seq"), None),
            P(("grp", "seq"), None),
            P(("grp", "seq"), None),
            P("grp", "seq"),
            P("grp", "seq"),
            P("grp"),
            P("grp"),
            P(),
        ),
        out_specs=P(("grp", "seq"), None),
        check_vma=False,
    )
```

```python
import functools
import math

import jax
import jax.numpy as jnp
from jax import lax
from jax.experimental import pallas as pl
from jax.experimental.pallas import tpu as pltpu
from jax.sharding import PartitionSpec as P


HD = 128
TO_LOG2 = HD ** (-0.5) * math.log2(math.e)
NT = (((1,), (1,)), ((), ()))

ANY = pl.BlockSpec(memory_space=pl.ANY)
WHOLE = pl.BlockSpec(memory_space=pltpu.VMEM)
SCALARS = pl.BlockSpec(memory_space=pltpu.SMEM)


def pack_body(slots, n_in, scal_ref, *refs):
    ins, outs = refs[:n_in], refs[n_in:]
    rows = ins[0].shape[0]
    width = outs[0].shape[1]
    for slot, out_ref in zip(slots, outs):
        at = pl.multiple_of((scal_ref[0] ^ slot) * width, HD)
        for place, ref in enumerate(ins):
            out_ref[place * rows : (place + 1) * rows] = ref[:, pl.ds(at, width)]


def pack(scal, arrays, slots, width):
    rows = arrays[0].shape[0]
    block = jax.ShapeDtypeStruct((len(arrays) * rows, width), arrays[0].dtype)
    return pl.pallas_call(
        functools.partial(pack_body, tuple(slots), len(arrays)),
        out_shape=[block] * len(slots),
        in_specs=[SCALARS] + [WHOLE] * len(arrays),
        out_specs=[WHOLE] * len(slots),
        cost_estimate=pl.CostEstimate(
            flops=0, bytes_accessed=4 * len(arrays) * arrays[0].size, transcendentals=0
        ),
    )(scal, *arrays)


def softmax_part(q, keys, values, head):
    cols = slice(head * HD, (head + 1) * HD)
    total = keys.shape[0]
    chunk = min(512, total)
    ones = jnp.ones((chunk, HD), jnp.bfloat16)
    top, acc = None, None
    for at in range(0, total, chunk):
        k = keys[at : at + chunk, cols]
        v = jnp.concatenate([values[at : at + chunk, cols], ones], axis=1)
        s = lax.dot_general(q, k, NT, preferred_element_type=jnp.float32)
        chunk_top = jnp.max(s, axis=1, keepdims=True)
        new_top = chunk_top if top is None else jnp.maximum(top, chunk_top)
        p = jnp.exp2((s - new_top) * TO_LOG2).astype(jnp.bfloat16)
        part = jnp.dot(p, v, preferred_element_type=jnp.float32)
        if top is None:
            acc = part
        else:
            acc = acc * jnp.exp2((top - new_top) * TO_LOG2) + part
        top = new_top
    return top, acc


def main_body(n_q, n_three, n_kv, scal_ref, *refs):
    three, only_q, only_kv = (
        refs[:n_three],
        refs[n_three : n_three + n_q],
        refs[n_three + n_q : n_three + n_q + n_kv],
    )
    rest = refs[n_three + n_q + n_kv :]
    stale_k, stale_v, acc_ref, stat_ref, q_ref, queries, keys, values, low_k, low_v, sems = rest
    rows = three[0].shape[0] // 3
    heads_dev = queries.shape[1] // HD
    patch = (n_three + n_q) * rows
    n_old = keys.shape[0] - (n_three + n_kv) * rows
    start = scal_ref[1]
    edge = pl.multiple_of(jnp.minimum(start // rows, n_old // rows - 1) * rows, rows)

    @pl.when(pl.program_id(0) == 0)
    def _():
        copies = []

        def take(src, dst):
            copies.append(pltpu.make_async_copy(src, dst, sems.at[len(copies)]))
            copies[-1].start()

        for at in range(0, n_old, rows):
            src = pl.multiple_of(jnp.where(at + rows <= start, at, at + patch), rows)
            take(stale_k.at[pl.ds(src, rows)], keys.at[pl.ds(at, rows)])
            take(stale_v.at[pl.ds(src, rows)], values.at[pl.ds(at, rows)])
        take(stale_k.at[pl.ds(edge, rows)], low_k)
        take(stale_v.at[pl.ds(edge, rows)], low_v)
        at = n_old
        for place, ref in enumerate(three):
            take(ref.at[pl.ds(0, rows)], queries.at[pl.ds(place * rows, rows)])
            take(ref.at[pl.ds(rows, rows)], keys.at[pl.ds(at, rows)])
            take(ref.at[pl.ds(2 * rows, rows)], values.at[pl.ds(at, rows)])
            at += rows
        for place, ref in enumerate(only_q):
            take(ref, queries.at[pl.ds((n_three + place) * rows, rows)])
        for ref in only_kv:
            take(ref.at[pl.ds(0, rows)], keys.at[pl.ds(at, rows)])
            take(ref.at[pl.ds(rows, rows)], values.at[pl.ds(at, rows)])
            at += rows
        for copy in copies:
            copy.wait()
        row = lax.broadcasted_iota(jnp.int32, low_k.shape, 0) + edge
        for low, full in ((low_k, keys), (low_v, values)):
            here = full.at[pl.ds(edge, rows)]
            kept = jnp.where(
                row < start, low[...].astype(jnp.float32), here[...].astype(jnp.float32)
            )
            here[...] = kept.astype(jnp.bfloat16)

    step_rows = q_ref.shape[0]
    base = pl.multiple_of(pl.program_id(0) * step_rows, step_rows)
    q_all = queries[pl.ds(base, step_rows), :]
    q_ref[...] = q_all
    block = min(256, step_rows)
    lane = lax.broadcasted_iota(jnp.int32, (block, HD), 1)
    for at in range(0, step_rows, block):
        for head in range(heads_dev):
            cols = slice(head * HD, (head + 1) * HD)
            q = q_all[at : at + block, cols]
            top, acc = softmax_part(q, keys, values, head)
            acc_ref[at : at + block, cols] = acc[:, :HD]
            stat_ref[at : at + block, cols] = jnp.where(lane < HD // 2, top, acc[:, HD:])


def attend_main(scal, three, only_q, only_kv, stale_k, stale_v):
    rows, width = three[0].shape[0] // 3, three[0].shape[1]
    patch = (len(three) + len(only_q)) * rows
    n_old = stale_k.shape[0] - patch
    total = n_old + (len(three) + len(only_kv)) * rows
    step = min(512, patch)
    n_copies = 2 * (n_old // rows) + 2 + 3 * len(three) + len(only_q) + 2 * len(only_kv)
    operands = (*three, *only_q, *only_kv, stale_k, stale_v)
    out = pl.BlockSpec((step, width), lambda i, s: (i, 0))
    return pl.pallas_call(
        functools.partial(main_body, len(only_q), len(three), len(only_kv)),
        out_shape=[
            jax.ShapeDtypeStruct((patch, width), jnp.float32),
            jax.ShapeDtypeStruct((patch, width), jnp.float32),
            jax.ShapeDtypeStruct((patch, width), jnp.bfloat16),
        ],
        grid_spec=pltpu.PrefetchScalarGridSpec(
            num_scalar_prefetch=1,
            grid=(patch // step,),
            in_specs=[ANY] * len(operands),
            out_specs=[out] * 3,
            scratch_shapes=[
                pltpu.VMEM((patch, width), jnp.bfloat16),
                pltpu.VMEM((total, width), jnp.bfloat16),
                pltpu.VMEM((total, width), jnp.bfloat16),
                pltpu.VMEM((rows, width), jnp.bfloat16),
                pltpu.VMEM((rows, width), jnp.bfloat16),
                pltpu.SemaphoreType.DMA((n_copies,)),
            ],
        ),
        cost_estimate=pl.CostEstimate(
            flops=6 * patch * total * width,
            bytes_accessed=2 * width * (6 * patch + 2 * total),
            transcendentals=patch * total * (width // HD),
        ),
    )(scal, *operands)


def last_body(n_kv, n_slots, scal_ref, *refs):
    kv_refs = refs[:n_kv]
    acc_ref, stat_ref, q_ref, gate_ref = refs[n_kv : n_kv + 4]
    out_refs = refs[n_kv + 4 : n_kv + 4 + n_slots]
    keys, values, sems = refs[n_kv + 4 + n_slots :]
    rows = out_refs[0].shape[0]
    heads_dev = q_ref.shape[1] // HD
    step_id = pl.program_id(0)

    @pl.when(step_id == 0)
    def _():
        copies = []
        for place, ref in enumerate(kv_refs):
            for half, full in enumerate((keys, values)):
                src = ref.at[pl.ds(half * rows, rows)]
                dst = full.at[pl.ds(place * rows, rows)]
                copies.append(pltpu.make_async_copy(src, dst, sems.at[len(copies)]))
                copies[-1].start()
        for copy in copies:
            copy.wait()

    gate = gate_ref[pl.ds(scal_ref[2], 1), :]
    step_rows = q_ref.shape[0]
    per = step_rows // rows
    block = min(256, step_rows)
    pieces = []
    for at in range(0, step_rows, block):
        heads = []
        for head in range(heads_dev):
            cols = slice(head * HD, (head + 1) * HD)
            here = slice(at, at + block)
            top, acc = softmax_part(q_ref[here, cols], keys, values, head)
            old_top = stat_ref[here, head * HD : head * HD + 1]
            old_sum = stat_ref[here, (head + 1) * HD - 1 : (head + 1) * HD]
            new_top = jnp.maximum(top, old_top)
            scale = jnp.exp2((top - new_top) * TO_LOG2)
            old_scale = jnp.exp2((old_top - new_top) * TO_LOG2)
            numer = acc[:, :HD] * scale + acc_ref[here, cols] * old_scale
            denom = acc[:, HD:] * scale + old_sum * old_scale
            attn = (numer / denom).astype(jnp.bfloat16)
            heads.append((attn.astype(jnp.float32) * gate[:, cols]).astype(jnp.bfloat16))
        gated = jnp.concatenate(heads, axis=1)
        pieces += [gated[i : i + rows] for i in range(0, block, rows)]
    for turn in range(n_slots // per):

        @pl.when(step_id == turn)
        def _():
            for place in range(per):
                out_refs[turn * per + place][...] = pieces[place]


def attend_last(scal, only_kv, acc, stat, queries, gate_table):
    rows, width = only_kv[0].shape[0] // 2, only_kv[0].shape[1]
    patch = queries.shape[0]
    total = len(only_kv) * rows
    step = min(512, patch)
    n_slots = patch // rows
    state = pl.BlockSpec((step, width), lambda i, s: (i, 0))
    gate = pl.BlockSpec((gate_table.shape[0], width), lambda i, s: (0, s[0]))
    piece = jax.ShapeDtypeStruct((rows, width), jnp.bfloat16)
    return pl.pallas_call(
        functools.partial(last_body, len(only_kv), n_slots),
        out_shape=[piece] * n_slots,
        grid_spec=pltpu.PrefetchScalarGridSpec(
            num_scalar_prefetch=1,
            grid=(patch // step,),
            in_specs=[ANY] * len(only_kv) + [state, state, state, gate],
            out_specs=[pl.BlockSpec((rows, width), lambda i, s: (0, 0))] * n_slots,
            scratch_shapes=[
                pltpu.VMEM((total, width), jnp.bfloat16),
                pltpu.VMEM((total, width), jnp.bfloat16),
                pltpu.SemaphoreType.DMA((2 * len(only_kv),)),
            ],
        ),
        cost_estimate=pl.CostEstimate(
            flops=6 * patch * total * width,
            bytes_accessed=2 * width * (6 * patch + 2 * total),
            transcendentals=patch * total * (width // HD),
        ),
    )(scal, *only_kv, acc, stat, queries, gate_table)


def unpack_body(scal_ref, *refs):
    out_ref = refs[-1]
    width = refs[0].shape[1]
    for slot, ref in enumerate(refs[:-1]):
        at = pl.multiple_of((scal_ref[0] ^ slot) * width, HD)
        out_ref[:, pl.ds(at, width)] = ref[...]


def unpack(scal, parts):
    rows, width = parts[0].shape
    return pl.pallas_call(
        unpack_body,
        out_shape=jax.ShapeDtypeStruct((rows, len(parts) * width), parts[0].dtype),
        in_specs=[SCALARS] + [WHOLE] * len(parts),
        out_specs=WHOLE,
    )(scal, *parts)


def shards(
    fresh_query, fresh_key, fresh_value, stale_key, stale_value, patch_start, timestep, gate_table
):
    n = lax.axis_size("seq")
    width = stale_key.shape[1]
    me = lax.axis_index("seq").astype(jnp.int32)
    near, far = range(n // 2), range(n // 2, n)

    def send(slot, block):
        return lax.ppermute(block, "seq", [(i, i ^ slot) for i in range(n)])

    def send_all(slots, blocks):
        return [b if s == 0 else send(s, b) for s, b in zip(slots, blocks)]

    scal = jnp.stack([me, patch_start[0], timestep[0]])
    q_blocks = pack(me[None], (fresh_query,), far, width)
    far_q = send_all(far, q_blocks)
    kv_blocks = pack(me[None], (fresh_key, fresh_value), far, width)
    far_kv = send_all(far, kv_blocks)
    near_blocks = pack(me[None], (fresh_query, fresh_key, fresh_value), near, width)
    three = send_all(near, near_blocks)
    early = len(far) // 2
    acc, stat, queries = attend_main(scal, three, far_q, far_kv[:early], stale_key, stale_value)
    outs = attend_last(scal, far_kv[early:], acc, stat, queries, gate_table)
    home_far = send_all(far, outs[n // 2 :])
    home_near = send_all(near, outs[: n // 2])
    return unpack(me[None], [*home_near, *home_far])


def solution(mesh):
    return jax.shard_map(
        shards,
        mesh=mesh,
        in_specs=(
            P(("grp", "seq"), None),
            P(("grp", "seq"), None),
            P(("grp", "seq"), None),
            P("grp", "seq"),
            P("grp", "seq"),
            P("grp"),
            P("grp"),
            P(),
        ),
        out_specs=P(("grp", "seq"), None),
        check_vma=False,
    )
```

```python
import functools
import math

import jax
import jax.numpy as jnp
from jax import lax
from jax.experimental import pallas as pl
from jax.experimental.pallas import tpu as pltpu
from jax.sharding import PartitionSpec as P


HD = 128
TO_LOG2 = HD ** (-0.5) * math.log2(math.e)
NT = (((1,), (1,)), ((), ()))

IN_HBM = pl.BlockSpec(memory_space=pltpu.HBM)
WHOLE = pl.BlockSpec(memory_space=pltpu.VMEM)
SCALARS = pl.BlockSpec(memory_space=pltpu.SMEM)


def run_copies(pairs, sems):
    copies = [
        pltpu.make_async_copy(src, dst, sems.at[i]) for i, (src, dst) in enumerate(pairs)
    ]
    for copy in copies:
        copy.start()
    for copy in copies:
        copy.wait()


def spread_body(x_ref, out_ref, sems):
    n, _, width = out_ref.shape
    run_copies(
        [(x_ref.at[:, pl.ds(dest * width, width)], out_ref.at[dest]) for dest in range(n)], sems
    )


def spread(x, n, width):
    return pl.pallas_call(
        spread_body,
        out_shape=jax.ShapeDtypeStruct((n, x.shape[0], width), x.dtype),
        in_specs=[IN_HBM],
        out_specs=WHOLE,
        scratch_shapes=[pltpu.SemaphoreType.DMA((n,))],
    )(x)


def pack_body(slots, scal_ref, k_ref, v_ref, *refs):
    outs, sems = refs[:-1], refs[-1]
    rows = k_ref.shape[0]
    width = outs[0].shape[1]
    pairs = []
    for slot, out_ref in zip(slots, outs):
        cols = pl.ds(pl.multiple_of((scal_ref[0] ^ slot) * width, HD), width)
        pairs.append((k_ref.at[:, cols], out_ref.at[pl.ds(0, rows)]))
        pairs.append((v_ref.at[:, cols], out_ref.at[pl.ds(rows, rows)]))
    run_copies(pairs, sems)


def pack(scal, k, v, slots, width):
    rows = k.shape[0]
    block = jax.ShapeDtypeStruct((2 * rows, width), k.dtype)
    return pl.pallas_call(
        functools.partial(pack_body, tuple(slots)),
        out_shape=[block] * len(slots),
        in_specs=[SCALARS, IN_HBM, IN_HBM],
        out_specs=[WHOLE] * len(slots),
        scratch_shapes=[pltpu.SemaphoreType.DMA((2 * len(slots),))],
    )(scal, k, v)


def softmax_add(queries, tops, accs, take_keys, take_values, total, limit):
    chunk = math.gcd(limit, total)
    ones = jnp.ones((chunk, HD), jnp.bfloat16)
    every = range(len(queries))
    for at in range(0, total, chunk):
        scores = [
            lax.dot_general(
                queries[i], take_keys(i, at, chunk), NT, preferred_element_type=jnp.float32
            )
            for i in every
        ]
        new_tops = [jnp.max(s, axis=1, keepdims=True) for s in scores]
        if tops is not None:
            new_tops = [jnp.maximum(new, old) for new, old in zip(new_tops, tops)]
        probs = [
            jnp.exp2((s - top) * TO_LOG2).astype(jnp.bfloat16)
            for s, top in zip(scores, new_tops)
        ]
        parts = [
            jnp.dot(
                probs[i],
                jnp.concatenate([take_values(i, at, chunk), ones], axis=1),
                preferred_element_type=jnp.float32,
            )
            for i in every
        ]
        if accs is not None:
            parts = [
                acc * jnp.exp2((old - new) * TO_LOG2) + part
                for acc, old, new, part in zip(accs, tops, new_tops, parts)
            ]
        tops, accs = new_tops, parts
    return tops, accs


def split_stat(stat):
    first = lax.broadcasted_iota(jnp.int32, stat.shape, 1) < HD // 2
    top = jnp.max(jnp.where(first, stat, -jnp.inf), axis=1, keepdims=True)
    row_sum = jnp.max(jnp.where(first, 0.0, stat), axis=1, keepdims=True)
    return top, jnp.broadcast_to(row_sum, stat.shape)


def stage_body(n_kv, has_stale, has_state, scal_ref, q_ref, *refs):
    refs = list(refs)
    take_refs = lambda count: [refs.pop(0) for _ in range(count)]
    state_in = take_refs(2 * has_state)
    kv_refs = take_refs(n_kv)
    stale = take_refs(2 * has_stale)
    acc_ref, stat_ref, keys, values, low_k, low_v, sems = refs
    per, rows, width = q_ref.shape
    total = keys.shape[0]
    n_old = total - n_kv * rows

    @pl.when(pl.program_id(0) == 0)
    def _():
        pairs = []
        for place, ref in enumerate(kv_refs):
            to = pl.ds(n_old + place * rows, rows)
            pairs.append((ref.at[pl.ds(0, rows)], keys.at[to]))
            pairs.append((ref.at[pl.ds(rows, rows)], values.at[to]))
        if has_stale:
            patch = stale[0].shape[0] - n_old
            start = scal_ref[1]
            edge = pl.multiple_of(jnp.minimum(start // rows, n_old // rows - 1) * rows, rows)
            for at in range(0, n_old, rows):
                src = pl.multiple_of(jnp.where(at + rows <= start, at, at + patch), rows)
                for ref, full in zip(stale, (keys, values)):
                    pairs.append((ref.at[pl.ds(src, rows)], full.at[pl.ds(at, rows)]))
            for ref, low in zip(stale, (low_k, low_v)):
                pairs.append((ref.at[pl.ds(edge, rows)], low))
        run_copies(pairs, sems)
        if has_stale:
            row = lax.broadcasted_iota(jnp.int32, low_k.shape, 0) + edge
            for low, full in ((low_k, keys), (low_v, values)):
                here = full.at[pl.ds(edge, rows)]
                kept = jnp.where(
                    row < start, low[...].astype(jnp.float32), here[...].astype(jnp.float32)
                )
                here[...] = kept.astype(jnp.bfloat16)

    q_all = q_ref[...].reshape(per * rows, width)
    block = min(256, per * rows)
    lane = lax.broadcasted_iota(jnp.int32, (block, HD), 1)
    for at in range(0, per * rows, block):
        here = slice(at, at + block)
        for cols in [slice(col, col + HD) for col in range(0, width, HD)]:
            tops, accs = None, None
            if has_state:
                top, row_sum = split_stat(state_in[1][here, cols])
                tops = [top]
                accs = [jnp.concatenate([state_in[0][here, cols], row_sum], axis=1)]
            (top,), (acc,) = softmax_add(
                [q_all[here, cols]],
                tops,
                accs,
                lambda i, at, chunk, cols=cols: keys[at : at + chunk, cols],
                lambda i, at, chunk, cols=cols: values[at : at + chunk, cols],
                total,
                1024 if has_state else 512,
            )
            acc_ref[here, cols] = acc[:, :HD]
            stat_ref[here, cols] = jnp.where(lane < HD // 2, top, acc[:, HD:])


def cost(patch, total, width):
    return pl.CostEstimate(
        flops=6 * patch * total * width,
        bytes_accessed=2 * width * (6 * patch + 2 * total),
        transcendentals=patch * total * (width // HD),
    )


def attend_stage(scal, queries, state, kv, stale):
    n, rows, width = queries.shape
    patch = n * rows
    n_old = stale[0].shape[0] - patch if stale else 0
    total = n_old + len(kv) * rows
    per = min(4, n)
    kept = jax.ShapeDtypeStruct((patch, width), jnp.float32)
    block = pl.BlockSpec((per * rows, width), lambda i, s: (i, 0))
    full = pltpu.VMEM((total, width), jnp.bfloat16)
    low = pltpu.VMEM((rows, width), jnp.bfloat16)
    n_copies = 2 * (total // rows + 1)
    return pl.pallas_call(
        functools.partial(stage_body, len(kv), bool(stale), bool(state)),
        out_shape=[kept, kept],
        grid_spec=pltpu.PrefetchScalarGridSpec(
            num_scalar_prefetch=1,
            grid=(n // per,),
            in_specs=[pl.BlockSpec((per, rows, width), lambda i, s: (i, 0, 0))]
            + [block] * len(state)
            + [IN_HBM] * (len(kv) + len(stale)),
            out_specs=[block, block],
            scratch_shapes=[full, full, low, low, pltpu.SemaphoreType.DMA((n_copies,))],
        ),
        cost_estimate=cost(patch, total, width),
    )(scal, queries, *state, *kv, *stale)


def last_body(n_kv, n, scal_ref, *refs):
    kv_refs = refs[:n_kv]
    q_hbm, acc_hbm, stat_hbm, gate_hbm = refs[n_kv : n_kv + 4]
    out_refs = refs[n_kv + 4 : n_kv + 4 + n]
    q_ref, acc_ref, stat_ref, gate_ref, keys, values, sems = refs[n_kv + 4 + n :]
    rows, width = out_refs[0].shape
    me = scal_ref[0]
    at = pl.multiple_of(me * width, HD)
    gate_copy = pltpu.make_async_copy(gate_hbm.at[:, pl.ds(at, width)], gate_ref, sems.at[3 * n])
    kv_copies = []
    for place, ref in enumerate(kv_refs):
        to = pl.ds(place * rows, rows)
        for half, full in enumerate((keys, values)):
            sem = sems.at[3 * n + 1 + len(kv_copies)]
            kv_copies.append(
                pltpu.make_async_copy(ref.at[pl.ds(half * rows, rows)], full.at[to], sem)
            )
            kv_copies[-1].start()
    copies = []
    for slot in range(n):
        source = me ^ slot
        place = pl.ds(pl.multiple_of(source * rows, rows), rows)
        to = pl.ds(slot * rows, rows)
        copies += [
            pltpu.make_async_copy(q_hbm.at[source], q_ref.at[to], sems.at[3 * slot]),
            pltpu.make_async_copy(acc_hbm.at[place], acc_ref.at[to], sems.at[3 * slot + 1]),
            pltpu.make_async_copy(stat_hbm.at[place], stat_ref.at[to], sems.at[3 * slot + 2]),
        ]
        for copy in copies[-3:]:
            copy.start()
        if slot == 1:
            gate_copy.start()
    head_cols = [slice(at, at + HD) for at in range(0, width, HD)]

    for copy in kv_copies:
        copy.wait()
    gate = None
    for first in range(0, n, 2):
        for copy in copies[3 * first : 3 * first + 6]:
            copy.wait()
        if gate is None:
            gate_copy.wait()
            gate = gate_ref[pl.ds(scal_ref[2], 1), :]
        here = slice(first * rows, (first + 2) * rows)
        for cols in head_cols:
            top, row_sum = split_stat(stat_ref[here, cols])
            _, (acc,) = softmax_add(
                [q_ref[here, cols]],
                [top],
                [jnp.concatenate([acc_ref[here, cols], row_sum], axis=1)],
                lambda i, at, chunk, cols=cols: keys[at : at + chunk, cols],
                lambda i, at, chunk, cols=cols: values[at : at + chunk, cols],
                n_kv * rows,
                1024,
            )
            attn = (acc[:, :HD] / acc[:, HD:]).astype(jnp.bfloat16)
            gated = (attn.astype(jnp.float32) * gate[:, cols]).astype(jnp.bfloat16)
            out_refs[first][:, cols] = gated[:rows]
            out_refs[first + 1][:, cols] = gated[rows:]


def attend_last(scal, queries, state, kv, gate_table):
    n, rows, width = queries.shape
    piece = jax.ShapeDtypeStruct((rows, width), jnp.bfloat16)
    kept = pltpu.VMEM((n * rows, width), jnp.float32)
    full = pltpu.VMEM((len(kv) * rows, width), jnp.bfloat16)
    return pl.pallas_call(
        functools.partial(last_body, len(kv), n),
        out_shape=[piece] * n,
        in_specs=[SCALARS] + [IN_HBM] * (len(kv) + 4),
        out_specs=[WHOLE] * n,
        scratch_shapes=[
            pltpu.VMEM((n * rows, width), jnp.bfloat16),
            kept,
            kept,
            pltpu.VMEM((gate_table.shape[0], width), jnp.float32),
            full,
            full,
            pltpu.SemaphoreType.DMA((3 * n + 1 + 2 * len(kv),)),
        ],
        cost_estimate=cost(n * rows, len(kv) * rows, width),
    )(scal, *kv, queries, *state, gate_table)


def unpack_body(scal_ref, *refs):
    parts, out_ref, sems = refs[:-2], refs[-2], refs[-1]
    width = parts[0].shape[1]
    pairs = []
    for slot, ref in enumerate(parts):
        at = pl.multiple_of((scal_ref[0] ^ slot) * width, HD)
        pairs.append((ref, out_ref.at[:, pl.ds(at, width)]))
    run_copies(pairs, sems)


def unpack(scal, parts):
    rows, width = parts[0].shape
    return pl.pallas_call(
        unpack_body,
        out_shape=jax.ShapeDtypeStruct((rows, len(parts) * width), parts[0].dtype),
        in_specs=[SCALARS] + [IN_HBM] * len(parts),
        out_specs=WHOLE,
        scratch_shapes=[pltpu.SemaphoreType.DMA((len(parts),))],
    )(scal, *parts)


def shards(
    fresh_query, fresh_key, fresh_value, stale_key, stale_value, patch_start, timestep, gate_table
):
    n = lax.axis_size("seq")
    width = stale_key.shape[1]
    me = lax.axis_index("seq").astype(jnp.int32)
    near, far = range(n // 2), range(n // 2, n)

    def send(slot, block):
        return lax.ppermute(block, "seq", [(i, i ^ slot) for i in range(n)])

    def send_all(slots, blocks):
        return [b if s == 0 else send(s, b) for s, b in zip(slots, blocks)]

    scal = jnp.stack([me, patch_start[0], timestep[0]])
    head, tail = far[: n // 8], far[n // 8 :]
    head_blocks = pack(me[None], fresh_key, fresh_value, head, width)
    head_kv = send_all(head, head_blocks)
    spread_q = spread(fresh_query, n, width)
    queries = lax.all_to_all(spread_q, "seq", 0, 0, tiled=True)
    blocks = pack(me[None], fresh_key, fresh_value, (*near, *tail), width)
    near_kv = send_all(near, blocks[: n // 2])
    tail_kv = send_all(tail, blocks[n // 2 :])
    state = attend_stage(scal, queries, [], head_kv, [stale_key, stale_value])
    state = attend_stage(scal, queries, state, near_kv, [])
    outs = attend_last(scal, queries, state, tail_kv, gate_table)
    home_far = send_all(far, outs[n // 2 :])
    home_near = send_all(near, outs[: n // 2])
    return unpack(me[None], [*home_near, *home_far])


def solution(mesh):
    return jax.shard_map(
        shards,
        mesh=mesh,
        in_specs=(
            P(("grp", "seq"), None),
            P(("grp", "seq"), None),
            P(("grp", "seq"), None),
            P("grp", "seq"),
            P("grp", "seq"),
            P("grp"),
            P("grp"),
            P(),
        ),
        out_specs=P(("grp", "seq"), None),
        check_vma=False,
    )
```

```python
import functools
import math

import jax
import jax.numpy as jnp
from jax import lax
from jax.experimental import pallas as pl
from jax.experimental.pallas import tpu as pltpu
from jax.sharding import PartitionSpec as P


HD = 128
TO_LOG2 = HD ** (-0.5) * math.log2(math.e)
NT = (((1,), (1,)), ((), ()))

LIMIT = 512
GROUP = 4
IN_HBM = pl.BlockSpec(memory_space=pltpu.HBM)
WHOLE = pl.BlockSpec(memory_space=pltpu.VMEM)
SCALARS = pl.BlockSpec(memory_space=pltpu.SMEM)


def run_copies(pairs, sems):
    copies = [
        pltpu.make_async_copy(src, dst, sems.at[i]) for i, (src, dst) in enumerate(pairs)
    ]
    for copy in copies:
        copy.start()
    for copy in copies:
        copy.wait()


def spread_body(x_ref, out_ref, sems):
    n, _, width = out_ref.shape
    run_copies(
        [(x_ref.at[:, pl.ds(dest * width, width)], out_ref.at[dest]) for dest in range(n)], sems
    )


def spread(x, n, width):
    return pl.pallas_call(
        spread_body,
        out_shape=jax.ShapeDtypeStruct((n, x.shape[0], width), x.dtype),
        in_specs=[IN_HBM],
        out_specs=WHOLE,
        scratch_shapes=[pltpu.SemaphoreType.DMA((n,))],
    )(x)


def pack_body(slots, scal_ref, k_ref, v_ref, *refs):
    outs, sems = refs[:-1], refs[-1]
    rows = k_ref.shape[0]
    width = outs[0].shape[1]
    pairs = []
    for slot, out_ref in zip(slots, outs):
        cols = pl.ds(pl.multiple_of((scal_ref[0] ^ slot) * width, HD), width)
        pairs.append((k_ref.at[:, cols], out_ref.at[pl.ds(0, rows)]))
        pairs.append((v_ref.at[:, cols], out_ref.at[pl.ds(rows, rows)]))
    run_copies(pairs, sems)


def pack(scal, k, v, slots, width):
    rows = k.shape[0]
    block = jax.ShapeDtypeStruct((2 * rows, width), k.dtype)
    return pl.pallas_call(
        functools.partial(pack_body, tuple(slots)),
        out_shape=[block] * len(slots),
        in_specs=[SCALARS, IN_HBM, IN_HBM],
        out_specs=[WHOLE] * len(slots),
        scratch_shapes=[pltpu.SemaphoreType.DMA((2 * len(slots),))],
    )(scal, k, v)


def softmax_add(queries, tops, accs, take_keys, take_values, total, limit):
    unit = math.gcd(256, total)
    chunk = max(c for c in range(unit, max(limit, unit) + 1, unit) if total % c == 0)
    ones = jnp.ones((chunk, HD), jnp.bfloat16)
    every = range(len(queries))
    for at in range(0, total, chunk):
        scores = [
            lax.dot_general(
                queries[i], take_keys(i, at, chunk), NT, preferred_element_type=jnp.float32
            )
            for i in every
        ]
        new_tops = [jnp.max(s, axis=1, keepdims=True) for s in scores]
        if tops is not None:
            new_tops = [jnp.maximum(new, old) for new, old in zip(new_tops, tops)]
        probs = [
            jnp.exp2((s - top) * TO_LOG2).astype(jnp.bfloat16)
            for s, top in zip(scores, new_tops)
        ]
        parts = [
            jnp.dot(
                probs[i],
                jnp.concatenate([take_values(i, at, chunk), ones], axis=1),
                preferred_element_type=jnp.float32,
            )
            for i in every
        ]
        if accs is not None:
            parts = [
                acc * jnp.exp2((old - new) * TO_LOG2) + part
                for acc, old, new, part in zip(accs, tops, new_tops, parts)
            ]
        tops, accs = new_tops, parts
    return tops, accs


def split_stat(stat):
    first = lax.broadcasted_iota(jnp.int32, stat.shape, 1) < HD // 2
    top = jnp.max(jnp.where(first, stat, -jnp.inf), axis=1, keepdims=True)
    row_sum = jnp.max(jnp.where(first, 0.0, stat), axis=1, keepdims=True)
    return top, jnp.broadcast_to(row_sum, stat.shape)


def stage_body(n_kv, has_stale, has_state, scal_ref, q_ref, *refs):
    refs = list(refs)
    take_refs = lambda count: [refs.pop(0) for _ in range(count)]
    state_in = take_refs(2 * has_state)
    kv_refs = take_refs(n_kv)
    stale = take_refs(2 * has_stale)
    acc_ref, stat_ref, keys, values, low_k, low_v, sems = refs
    per, rows, width = q_ref.shape
    total = keys.shape[0]
    n_old = total - n_kv * rows

    @pl.when(pl.program_id(0) == 0)
    def _():
        pairs = []
        for place, ref in enumerate(kv_refs):
            to = pl.ds(n_old + place * rows, rows)
            pairs.append((ref.at[pl.ds(0, rows)], keys.at[to]))
            pairs.append((ref.at[pl.ds(rows, rows)], values.at[to]))
        if has_stale:
            patch = stale[0].shape[0] - n_old
            start = scal_ref[1]
            edge = pl.multiple_of(jnp.minimum(start // rows, n_old // rows - 1) * rows, rows)
            for at in range(0, n_old, rows):
                src = pl.multiple_of(jnp.where(at + rows <= start, at, at + patch), rows)
                for ref, full in zip(stale, (keys, values)):
                    pairs.append((ref.at[pl.ds(src, rows)], full.at[pl.ds(at, rows)]))
            for ref, low in zip(stale, (low_k, low_v)):
                pairs.append((ref.at[pl.ds(edge, rows)], low))
        run_copies(pairs, sems)
        if has_stale:
            row = lax.broadcasted_iota(jnp.int32, low_k.shape, 0) + edge
            for low, full in ((low_k, keys), (low_v, values)):
                here = full.at[pl.ds(edge, rows)]
                kept = jnp.where(
                    row < start, low[...].astype(jnp.float32), here[...].astype(jnp.float32)
                )
                here[...] = kept.astype(jnp.bfloat16)

    q_all = q_ref[...].reshape(per * rows, width)
    block = min(256, per * rows)
    lane = lax.broadcasted_iota(jnp.int32, (block, HD), 1)
    for at in range(0, per * rows, block):
        here = slice(at, at + block)
        for cols in [slice(col, col + HD) for col in range(0, width, HD)]:
            tops, accs = None, None
            if has_state:
                top, row_sum = split_stat(state_in[1][here, cols])
                tops = [top]
                accs = [jnp.concatenate([state_in[0][here, cols], row_sum], axis=1)]
            (top,), (acc,) = softmax_add(
                [q_all[here, cols]],
                tops,
                accs,
                lambda i, at, chunk, cols=cols: keys[at : at + chunk, cols],
                lambda i, at, chunk, cols=cols: values[at : at + chunk, cols],
                total,
                LIMIT,
            )
            acc_ref[here, cols] = acc[:, :HD]
            stat_ref[here, cols] = jnp.where(lane < HD // 2, top, acc[:, HD:])


def cost(patch, total, width):
    return pl.CostEstimate(
        flops=6 * patch * total * width,
        bytes_accessed=2 * width * (6 * patch + 2 * total),
        transcendentals=patch * total * (width // HD),
    )


def attend_stage(scal, queries, state, kv, stale):
    n, rows, width = queries.shape
    patch = n * rows
    n_old = stale[0].shape[0] - patch if stale else 0
    total = n_old + len(kv) * rows
    per = min(4, n)
    kept = jax.ShapeDtypeStruct((patch, width), jnp.float32)
    block = pl.BlockSpec((per * rows, width), lambda i, s: (i, 0))
    full = pltpu.VMEM((total, width), jnp.bfloat16)
    low = pltpu.VMEM((rows, width), jnp.bfloat16)
    n_copies = 2 * (total // rows + 1)
    return pl.pallas_call(
        functools.partial(stage_body, len(kv), bool(stale), bool(state)),
        out_shape=[kept, kept],
        grid_spec=pltpu.PrefetchScalarGridSpec(
            num_scalar_prefetch=1,
            grid=(n // per,),
            in_specs=[pl.BlockSpec((per, rows, width), lambda i, s: (i, 0, 0))]
            + [block] * len(state)
            + [IN_HBM] * (len(kv) + len(stale)),
            out_specs=[block, block],
            scratch_shapes=[full, full, low, low, pltpu.SemaphoreType.DMA((n_copies,))],
        ),
        cost_estimate=cost(patch, total, width),
    )(scal, queries, *state, *kv, *stale)


def last_body(n_kv, n, scal_ref, *refs):
    kv_refs = refs[:n_kv]
    q_hbm, acc_hbm, stat_hbm, gate_hbm = refs[n_kv : n_kv + 4]
    out_refs = refs[n_kv + 4 : n_kv + 4 + n]
    q_ref, acc_ref, stat_ref, gate_ref, keys, values, pieces, sems = refs[n_kv + 4 + n :]
    rows, width = out_refs[0].shape
    me = scal_ref[0]
    at = pl.multiple_of(me * width, HD)
    gate_copy = pltpu.make_async_copy(gate_hbm.at[:, pl.ds(at, width)], gate_ref, sems.at[3 * n])
    kv_copies = []
    for place, ref in enumerate(kv_refs):
        to = pl.ds(place * rows, rows)
        for half, full in enumerate((keys, values)):
            sem = sems.at[3 * n + 1 + len(kv_copies)]
            kv_copies.append(
                pltpu.make_async_copy(ref.at[pl.ds(half * rows, rows)], full.at[to], sem)
            )
            kv_copies[-1].start()
    copies = []
    for slot in range(n):
        source = me ^ slot
        place = pl.ds(pl.multiple_of(source * rows, rows), rows)
        to = pl.ds(slot * rows, rows)
        copies += [
            pltpu.make_async_copy(q_hbm.at[source], q_ref.at[to], sems.at[3 * slot]),
            pltpu.make_async_copy(acc_hbm.at[place], acc_ref.at[to], sems.at[3 * slot + 1]),
            pltpu.make_async_copy(stat_hbm.at[place], stat_ref.at[to], sems.at[3 * slot + 2]),
        ]
        for copy in copies[-3:]:
            copy.start()
        if slot == 1:
            gate_copy.start()
    head_cols = [slice(at, at + HD) for at in range(0, width, HD)]

    for copy in kv_copies:
        copy.wait()
    gate, out_copies = None, []
    group = min(GROUP, n)
    for first in range(0, n, group):
        for copy in copies[3 * first : 3 * (first + group)]:
            copy.wait()
        if gate is None:
            gate_copy.wait()
            gate = gate_ref[pl.ds(scal_ref[2], 1), :]
        here = slice(first * rows, (first + group) * rows)
        for cols in head_cols:
            top, row_sum = split_stat(stat_ref[here, cols])
            _, (acc,) = softmax_add(
                [q_ref[here, cols]],
                [top],
                [jnp.concatenate([acc_ref[here, cols], row_sum], axis=1)],
                lambda i, at, chunk, cols=cols: keys[at : at + chunk, cols],
                lambda i, at, chunk, cols=cols: values[at : at + chunk, cols],
                n_kv * rows,
                LIMIT,
            )
            attn = (acc[:, :HD] / acc[:, HD:]).astype(jnp.bfloat16)
            gated = (attn.astype(jnp.float32) * gate[:, cols]).astype(jnp.bfloat16)
            for place in range(group):
                pieces[first + place, :, cols] = gated[place * rows : (place + 1) * rows]
        for slot in range(first, first + group):
            sem = sems.at[3 * n + 1 + len(kv_copies) + slot]
            out_copies.append(pltpu.make_async_copy(pieces.at[slot], out_refs[slot], sem))
            out_copies[-1].start()
    for copy in out_copies:
        copy.wait()


def attend_last(scal, queries, state, kv, gate_table):
    n, rows, width = queries.shape
    piece = jax.ShapeDtypeStruct((rows, width), jnp.bfloat16)
    kept = pltpu.VMEM((n * rows, width), jnp.float32)
    full = pltpu.VMEM((len(kv) * rows, width), jnp.bfloat16)
    return pl.pallas_call(
        functools.partial(last_body, len(kv), n),
        out_shape=[piece] * n,
        in_specs=[SCALARS] + [IN_HBM] * (len(kv) + 4),
        out_specs=[IN_HBM] * n,
        scratch_shapes=[
            pltpu.VMEM((n * rows, width), jnp.bfloat16),
            kept,
            kept,
            pltpu.VMEM((gate_table.shape[0], width), jnp.float32),
            full,
            full,
            pltpu.VMEM((n, rows, width), jnp.bfloat16),
            pltpu.SemaphoreType.DMA((4 * n + 1 + 2 * len(kv),)),
        ],
        cost_estimate=cost(n * rows, len(kv) * rows, width),
    )(scal, *kv, queries, *state, gate_table)


def unpack_body(scal_ref, *refs):
    parts, out_ref, sems = refs[:-2], refs[-2], refs[-1]
    width = parts[0].shape[1]
    pairs = []
    for slot, ref in enumerate(parts):
        at = pl.multiple_of((scal_ref[0] ^ slot) * width, HD)
        pairs.append((ref, out_ref.at[:, pl.ds(at, width)]))
    run_copies(pairs, sems)


def unpack(scal, parts):
    rows, width = parts[0].shape
    return pl.pallas_call(
        unpack_body,
        out_shape=jax.ShapeDtypeStruct((rows, len(parts) * width), parts[0].dtype),
        in_specs=[SCALARS] + [IN_HBM] * len(parts),
        out_specs=WHOLE,
        scratch_shapes=[pltpu.SemaphoreType.DMA((len(parts),))],
    )(scal, *parts)


def split_far(n):
    far, few = range(n // 2, n), max(1, n // 8)
    return far[:few], far[few:]


def shards(
    fresh_query, fresh_key, fresh_value, stale_key, stale_value, patch_start, timestep, gate_table
):
    n = lax.axis_size("seq")
    width = stale_key.shape[1]
    me = lax.axis_index("seq").astype(jnp.int32)
    near, far = range(n // 2), range(n // 2, n)

    def send(slot, block):
        return lax.ppermute(block, "seq", [(i, i ^ slot) for i in range(n)])

    def send_all(slots, blocks):
        return [b if s == 0 else send(s, b) for s, b in zip(slots, blocks)]

    scal = jnp.stack([me, patch_start[0], timestep[0]])
    head, tail = split_far(n)
    head_blocks = [
        jnp.concatenate(
            [
                lax.dynamic_slice_in_dim(x, (me ^ slot) * width, width, 1)
                for x in (fresh_key, fresh_value)
            ]
        )
        for slot in head
    ]
    head_kv = send_all(head, head_blocks)
    spread_q = spread(fresh_query, n, width)
    queries = lax.all_to_all(spread_q, "seq", 0, 0, tiled=True)
    blocks = pack(me[None], fresh_key, fresh_value, (*near, *tail), width)
    near_kv = send_all(near, blocks[: n // 2])
    tail_kv = send_all(tail, blocks[n // 2 :])
    state = attend_stage(scal, queries, [], head_kv, [stale_key, stale_value])
    state = attend_stage(scal, queries, state, near_kv, [])
    outs = attend_last(scal, queries, state, tail_kv, gate_table)
    home_far = send_all(far, outs[n // 2 :])
    home_near = send_all(near, outs[: n // 2])
    return unpack(me[None], [*home_near, *home_far])


def solution(mesh):
    return jax.shard_map(
        shards,
        mesh=mesh,
        in_specs=(
            P(("grp", "seq"), None),
            P(("grp", "seq"), None),
            P(("grp", "seq"), None),
            P("grp", "seq"),
            P("grp", "seq"),
            P("grp"),
            P("grp"),
            P(),
        ),
        out_specs=P(("grp", "seq"), None),
        check_vma=False,
    )
```
